256 devices in a mesh: ang: 32 (over y_hi, z, core), row: 8 (over x, y_lo).
Axes of the slice: x: 4, y: 4 (y_hi: 2, y_lo: 2; y = y_hi * 2 + y_lo), z: 8, core: 2. Of those that a mesh axis runs over, the one named last changes fastest.
Arguments:
- echoes: bfloat16 [1024, 2, 16384], P('ang', None, 'row'), may hold values from -6 to 6
- pulse_ids: int32 [64, 512], replicated, may hold values from 0 to 1023, as said below
- bin_start: int32 [64, 512], replicated, may hold values from 0 to 16256
- live_count: int32 [64, 32], replicated, may hold values from 1 to 16
- wavenum: int32 [1024], replicated, may hold values from 1 to 32767
- interp: bfloat16 [64, 128, 128], P('row'), may hold values from -0.5 to 0.5
Outputs:
- image: bfloat16 [32768, 2, 8192], P('ang', None, 'row')
The draws below stay inside these ranges and needn't reach their ends.
Inputs may be any that keep to these rules, and one draw needn't show every extreme that they name: `pulse_ids`: entries 16 * a to 16 * a + 15 of each tile name distinct pulses of aperture block a, numbered a * 32 to a * 32 + 31.
All inputs are finite; a program needn't handle non-finite values.
Results may differ from the reference program's by a relative error of at most 0.0055.
Values may be sent and summed in bfloat16 or wider, within the bound.
No kernel may reach another device: no remote copies, remote signals or barrier semaphores. Data moves between devices by JAX's collectives and lax.ppermute only.
A program may use at most 320 MiB of HBM per device.

```python
import math
import jax
import jax.numpy as jnp
from jax import lax

BINS = 16384
WIN = 128
TR = 128
COLS = 32768
P_ANG = 32
J_DEV = 16
PULSES = 1024
FOOT = 512
TILES = 64
ROWS = 8192
N_ANG = 32


def draw_pulse_ids(key, part):
    blocks = PULSES // P_ANG
    key_list = jax.random.split(key, TILES * blocks)

    def choose_block(sub_key):
        return jax.random.permutation(sub_key, P_ANG)[:J_DEV].astype(jnp.int32)
    chosen = jax.vmap(choose_block)(key_list)
    chosen = chosen.reshape(TILES, blocks, J_DEV) + (jnp.arange(blocks, dtype=jnp.int32) * P_ANG)[None, :, None]
    return chosen.reshape(TILES, FOOT).astype(jnp.int32)


def plant(drawn, stream_key, low, high):
    shape = drawn.shape
    spot = [jax.random.randint(jax.random.fold_in(stream_key, axis), (), 0, shape[axis]) for axis in range(len(shape))]
    drawn = drawn.at[tuple(spot)].set(low)
    longest = shape.index(max(shape))
    spot[longest] = (spot[longest] + 1) % shape[longest]
    return drawn.at[tuple(spot)].set(high)


def shard_levels(stream_key, dims, pieces, least, largest):
    loudness = 1.0
    for position, shards_of in pieces:
        heights = jax.random.uniform(jax.random.fold_in(jax.random.fold_in(stream_key, 6), position), (shards_of,), jnp.float32, least / len(pieces), largest / len(pieces))
        loudness = loudness * jnp.repeat(jnp.exp(heights), dims[position] // shards_of).reshape((-1,) + (1,) * (len(dims) - 1 - position))
    return loudness


def gaussian(key, extent, scale, limit, cuts=(), kind=jnp.bfloat16):
    entries = scale * jax.random.normal(key, extent, jnp.float32)
    if cuts:
        entries = entries * shard_levels(key, extent, cuts, -0.22, 0.18)
    return jnp.clip(entries, -limit, limit).astype(kind)


def setup_inputs(seed: int = 0) -> dict:
    arg_keys = jax.random.split(jax.random.key(seed), 7)
    echoes = gaussian(arg_keys[0], (PULSES, 2, BINS), 1.0, 6.0, ((0, 32), (2, 8)))
    pulse_ids = draw_pulse_ids(jax.random.fold_in(arg_keys[6], 71), 0)
    bin_start = plant(jax.random.randint(arg_keys[2], (TILES, FOOT), 0, BINS - WIN + 1), jax.random.fold_in(arg_keys[2], 1), 0, BINS - WIN).astype(jnp.int32)
    live_count = plant(jax.random.randint(arg_keys[3], (TILES, N_ANG), 1, J_DEV + 1), jax.random.fold_in(arg_keys[3], 1), 1, J_DEV).astype(jnp.int32)
    wavenum = plant(jax.random.randint(arg_keys[4], (PULSES,), 1, COLS), jax.random.fold_in(arg_keys[4], 1), 1, COLS - 1).astype(jnp.int32)
    interp = gaussian(arg_keys[5], (TILES, TR, WIN), WIN ** -0.5, 0.5, ((0, 8),))
    return dict(echoes=echoes, pulse_ids=pulse_ids, bin_start=bin_start, live_count=live_count, wavenum=wavenum, interp=interp)


def reference(echoes, pulse_ids, bin_start, live_count, wavenum, interp):
    slot_index = jnp.arange(FOOT, dtype=jnp.int32)
    kept_mask = (slot_index % J_DEV)[None, :] < live_count[:, slot_index // J_DEV]
    columns = jnp.arange(COLS, dtype=jnp.int32)
    step_angle = 2.0 * math.pi / COLS
    norm_scale = FOOT ** -0.5
    zero_index = jnp.zeros((), jnp.int32)

    def cut_panel(pulse, anchor):
        return lax.dynamic_slice(echoes, (pulse.astype(jnp.int32), zero_index, anchor.astype(jnp.int32)), (1, 2, WIN))[0]

    def one_tile(tile_args):
        tile_ids, starts, kept_rows, weights = tile_args
        panels = jax.vmap(cut_panel)(tile_ids, starts)
        panels = jnp.where(kept_rows[:, None, None], panels, jnp.zeros_like(panels))
        focused = jnp.einsum("ib,fcb->cfi", weights.astype(jnp.float32), panels.astype(jnp.float32)).astype(jnp.bfloat16)
        rate_rows = wavenum[tile_ids]
        phase_angle = ((rate_rows[:, None] * columns[None, :]) % COLS).astype(jnp.float32) * step_angle
        cosine = jnp.cos(phase_angle).astype(jnp.bfloat16)
        sine_part = jnp.sin(phase_angle).astype(jnp.bfloat16)
        real_part = jnp.dot(cosine.T, focused[0], preferred_element_type=jnp.float32) - jnp.dot(sine_part.T, focused[1], preferred_element_type=jnp.float32)
        imag_part = jnp.dot(sine_part.T, focused[0], preferred_element_type=jnp.float32) + jnp.dot(cosine.T, focused[1], preferred_element_type=jnp.float32)
        return (jnp.stack([real_part, imag_part], 1) * norm_scale).astype(jnp.bfloat16)

    tiles_out = lax.map(one_tile, (pulse_ids, bin_start, kept_mask, interp))
    return jnp.transpose(tiles_out, (1, 2, 0, 3)).reshape(COLS, 2, ROWS)
```

```python
import functools
import math

import jax
import jax.numpy as jnp
from jax import lax
from jax.experimental import pallas as pl
from jax.experimental.pallas import tpu as pltpu
from jax.sharding import Mesh
from jax.sharding import PartitionSpec as P

COLS = 32768
LANES = 128
ANG = ("yh", "z", "core")
ROW = ("x", "yl")
FINE = ("yh", "z", "core", "x", "yl")
GROUP = 8


def pack_kernel(low_ref, high_ref, bins_ref, offs_ref, out_ref, low_sc, high_sc, *, bins):
    windows = low_ref.shape[0]

    def take(step, _):
        for u in range(16):
            w = step * 16 + u
            lo = pl.multiple_of(low_ref[w], 2)
            hi = pl.multiple_of(high_ref[w], 2)
            at = pl.multiple_of(w * 2, 2)
            low_sc[pl.ds(at, 2), :] = bins_ref[pl.ds(lo, 2), :]
            high_sc[pl.ds(at, 2), :] = bins_ref[pl.ds(hi, 2), :]
        return 0

    lax.fori_loop(0, windows // 16, take, 0)
    lane = lax.broadcasted_iota(jnp.int32, (16, LANES), 1)

    def shift(step, _):
        for u in range(4):
            rows = pl.ds(pl.multiple_of((step * 4 + u) * 16, 16), 16)
            offs = offs_ref[rows, :]
            low = low_sc[rows, :]
            high = high_sc[rows, :]
            for bit in range(7):
                by = 1 << bit
                on = (offs & by) != 0
                low = jnp.where(on, pltpu.roll(low, LANES - by, 1), low)
                high = jnp.where(on, pltpu.roll(high, LANES - by, 1), high)
            here = offs + lane
            cut = jnp.where((offs & (LANES - 1)) + lane < LANES, low, high)
            cut = jnp.where((here >= 0) & (here < bins), cut, 0.0)
            out_ref[rows, :] = cut.astype(jnp.bfloat16)
        return 0

    lax.fori_loop(0, windows * 2 // 64, shift, 0)


def pack(echoes, ids, starts, live):
    pulses, parts, bins = echoes.shape
    panels = bins // LANES
    row_index = lax.axis_index(ROW)
    tiles, per_block = ids.shape
    windows = tiles * per_block
    rows = (
        echoes.astype(jnp.float32)
        .reshape(pulses, parts, panels, LANES)
        .transpose(0, 2, 1, 3)
        .reshape(pulses * panels * parts, LANES)
    )
    offs = starts - row_index * bins
    used = jnp.arange(per_block, dtype=jnp.int32)[None, :] < live[:, None]
    offs = jnp.where(used, offs, -2 * COLS).reshape(windows)
    panel = offs >> 7
    base = ids.reshape(windows) * (panels * parts)
    low = base + jnp.clip(panel, 0, panels - 1) * parts
    high = base + jnp.clip(panel + 1, 0, panels - 1) * parts
    spread = jnp.broadcast_to(offs[:, None, None], (windows, parts, LANES)).reshape(
        windows * parts, LANES
    )
    smem = pl.BlockSpec(memory_space=pltpu.SMEM)
    vmem = pl.BlockSpec(memory_space=pltpu.VMEM)
    return pl.pallas_call(
        functools.partial(pack_kernel, bins=bins),
        out_shape=jax.ShapeDtypeStruct((windows * parts, LANES), jnp.bfloat16),
        in_specs=[smem, smem, vmem, vmem],
        out_specs=vmem,
        scratch_shapes=[pltpu.VMEM((windows * parts, LANES), jnp.float32)] * 2,
        compiler_params=pltpu.CompilerParams(vmem_limit_bytes=24 << 20),
        name="pack",
    )(low, high, rows, spread)


def focus_kernel(got_ref, interp_ref, out_ref):
    tiles = interp_ref.shape[0]
    rows = out_ref.shape[0] // tiles
    panels = got_ref[0].astype(jnp.float32)
    for source in range(1, got_ref.shape[0]):
        panels += got_ref[source].astype(jnp.float32)
    panels = panels.astype(jnp.bfloat16)
    for tile in range(tiles):
        out_ref[tile * rows : (tile + 1) * rows, :] = lax.dot_general(
            panels[tile * rows : (tile + 1) * rows, :],
            interp_ref[tile],
            (((1,), (1,)), ((), ())),
            preferred_element_type=jnp.float32,
        ).astype(jnp.bfloat16)


def focus(got, interp):
    return pl.pallas_call(
        focus_kernel,
        out_shape=jax.ShapeDtypeStruct(got.shape[1:], jnp.bfloat16),
        in_specs=[pl.BlockSpec(memory_space=pltpu.VMEM)] * 2,
        out_specs=pl.BlockSpec(memory_space=pltpu.VMEM),
        name="focus",
    )(got, interp)


def image_kernel(*refs, tiles, scale):
    code_ref, cos_ref, sin_ref = refs[:3]
    blocks = refs[3:-2]
    out_ref, spread = refs[-2:]
    pulses = cos_ref.shape[1]
    half = spread.shape[0] // 2

    @pl.when(pl.program_id(0) == 0)
    def _():
        both = blocks[0].shape[0] // (blocks[0].shape[1] * 2)
        entry_rows = 32
        per = GROUP // 2
        slots = GROUP * 32
        row = lax.broadcasted_iota(jnp.int32, (2 * slots, GROUP * entry_rows), 0)
        for group in range(len(blocks) // per):
            for tile in range(tiles):
                parts = []
                for ref in blocks[group * per : (group + 1) * per]:
                    for side in range(2):
                        first = side * tiles * entry_rows + tile * entry_rows
                        parts.append(ref[first : first + entry_rows, :])
                stacked = jnp.concatenate(parts, 0)
                hot = row == code_ref[tile, group, :, :]
                hot = jnp.where(hot, 1.0, 0.0).astype(jnp.bfloat16)
                placed = jnp.dot(hot, stacked, preferred_element_type=jnp.float32).astype(jnp.bfloat16)
                columns = slice(tile * LANES, (tile + 1) * LANES)
                spread[group * slots : (group + 1) * slots, columns] = placed[:slots]
                spread[half + group * slots : half + (group + 1) * slots, columns] = placed[slots:]

    total = jnp.dot(cos_ref[...], spread[:half, :], preferred_element_type=jnp.float32)
    total += jnp.dot(sin_ref[...], spread[half:, :], preferred_element_type=jnp.float32)
    out_ref[...] = (total * scale).astype(jnp.bfloat16).reshape(out_ref.shape)


def image(code, cos, sin, blocks, tiles, scale):
    rows, pulses = cos.shape
    step = 256
    whole = pl.BlockSpec(memory_space=pltpu.VMEM)
    return pl.pallas_call(
        functools.partial(image_kernel, tiles=tiles, scale=scale),
        out_shape=jax.ShapeDtypeStruct((rows // 2, 2, tiles * LANES), jnp.bfloat16),
        grid=(rows // step,),
        in_specs=[whole]
        + [pl.BlockSpec((step, pulses), lambda i: (i, 0))] * 2
        + [whole] * len(blocks),
        out_specs=pl.BlockSpec((step // 2, 2, tiles * LANES), lambda i: (i, 0, 0)),
        scratch_shapes=[pltpu.VMEM((2 * pulses, tiles * LANES), jnp.bfloat16)],
        compiler_params=pltpu.CompilerParams(vmem_limit_bytes=40 << 20),
        name="image",
    )(code, cos, sin, *blocks)


def pick(table, index):
    hot = index[:, None] == jnp.arange(table.shape[0], dtype=jnp.int32)[None, :]
    wide = hot.reshape(hot.shape + (1,) * (table.ndim - 1))
    return jnp.sum(jnp.where(wide, table[None], 0), axis=1)


def twiddles(rates, first_column, columns):
    step_angle = 2.0 * math.pi / COLS
    fine = 32
    coarse_k = first_column + fine * jnp.arange(columns // fine, dtype=jnp.int32)
    coarse = ((rates[None, :] * coarse_k[:, None]) % COLS).astype(jnp.float32) * step_angle
    row = jnp.arange(2 * fine, dtype=jnp.int32)
    turn = rates[None, :] * (row // 2)[:, None] + (COLS - (COLS // 4) * (row % 2))[:, None]
    within = (turn % COLS).astype(jnp.float32) * step_angle
    coarse_c, coarse_s, fine_c, fine_s = lax.optimization_barrier(
        (jnp.cos(coarse), jnp.sin(coarse), jnp.cos(within), jnp.sin(within))
    )
    coarse_c, coarse_s = coarse_c[:, None, :], coarse_s[:, None, :]
    fine_c, fine_s = fine_c[None], fine_s[None]
    shape = (2 * columns, rates.shape[0])
    cos = (coarse_c * fine_c - coarse_s * fine_s).astype(jnp.bfloat16).reshape(shape)
    sin = (-coarse_s * fine_c - coarse_c * fine_s).astype(jnp.bfloat16).reshape(shape)
    return cos, sin


def body(echoes, pulse_ids, bin_start, live_count, wavenum, interp):
    blocks = lax.axis_size(ANG)
    ang_index = lax.axis_index(ANG)
    row_index = lax.axis_index(ROW)
    n_rows = lax.axis_size(ROW)
    ring = lax.axis_size("z")
    tiles_mine = interp.shape[0]
    block_pulses = echoes.shape[0]
    foot_len = pulse_ids.shape[1]
    per_block = foot_len // blocks
    col_dev = COLS // blocks
    first_entry = ang_index * per_block
    local_ids = pulse_ids % block_pulses

    my_ids = lax.dynamic_slice_in_dim(local_ids, first_entry, per_block, 1)
    my_starts = lax.dynamic_slice_in_dim(bin_start, first_entry, per_block, 1)
    my_live = lax.dynamic_slice_in_dim(live_count, ang_index, 1, 1)[:, 0]
    packed = pack(echoes, my_ids, my_starts, my_live)
    rows = packed.shape[0] // n_rows
    got = lax.all_to_all(packed.reshape(n_rows, rows, LANES), ROW, 0, 0, tiled=True)
    mine = focus(got, interp)

    swap = [(0, 1), (1, 0)]
    ahead = [(i, (i + 1) % ring) for i in range(ring)]
    behind = [(i, (i - 1) % ring) for i in range(ring)]
    other = lax.ppermute(mine, "yh", swap)
    block = jnp.concatenate([mine, other], 0)
    held = [block]
    shifts = [0]
    forward = backward = block
    for step in range(1, ring // 2 + 1):
        forward = lax.ppermute(forward, "z", ahead)
        held.append(forward)
        shifts.append(-step)
        if step < ring - step:
            backward = lax.ppermute(backward, "z", behind)
            held.append(backward)
            shifts.append(step)
    sibling = [lax.ppermute(b, "core", swap) for b in held]
    arrays, zs, cores = [], [], []
    for near, far, shift in zip(held, sibling, shifts):
        arrays += [near, far]
        zs += [shift, shift]
        cores += [0, 1]
    yh, z, core = (lax.axis_index(name) for name in ANG)
    at_z = (z + jnp.repeat(jnp.array(zs, jnp.int32), 2)) % ring
    at_core = core ^ jnp.repeat(jnp.array(cores, jnp.int32), 2)
    at_yh = yh ^ jnp.tile(jnp.array([0, 1], jnp.int32), len(arrays))
    order = (at_yh * ring + at_z) * 2 + at_core

    tile_ids = lax.dynamic_slice_in_dim(local_ids, row_index * tiles_mine, tiles_mine, 0)
    by_block = tile_ids.reshape(tiles_mine, blocks, per_block).transpose(1, 0, 2)
    placed = pick(by_block, order).transpose(1, 0, 2)
    placed = placed + block_pulses * (jnp.arange(blocks, dtype=jnp.int32) % GROUP)[None, :, None]
    code = placed[..., None] + GROUP * block_pulses * jnp.arange(2, dtype=jnp.int32)
    code = code.reshape(tiles_mine, blocks // GROUP, 1, GROUP * per_block * 2)
    rates = pick(wavenum.reshape(blocks, block_pulses), order).reshape(-1)
    cos, sin = twiddles(rates, ang_index * col_dev, col_dev)
    return image(code, cos, sin, arrays, tiles_mine, foot_len ** (-0.5))


def solution(mesh):
    finer = Mesh(mesh.devices.reshape(2, -1, 2, 4, 2), FINE)
    return jax.shard_map(
        body,
        mesh=finer,
        in_specs=(P(ANG, None, ROW), P(), P(), P(), P(), P(ROW, None, None)),
        out_specs=P(ANG, None, ROW),
        check_vma=False,
    )
```

```python
import functools
import math

import jax
import jax.numpy as jnp
from jax import lax
from jax.experimental import pallas as pl
from jax.experimental.pallas import tpu as pltpu
from jax.sharding import Mesh
from jax.sharding import PartitionSpec as P

COLS = 32768
LANES = 128
FINE_K = 32
ANG = ("yh", "z", "core")
ROW = ("x", "yl")
FINE = ("yh", "z", "core", "x", "yl")
SMEM = pl.BlockSpec(memory_space=pltpu.SMEM)
VMEM = pl.BlockSpec(memory_space=pltpu.VMEM)


def pack_kernel(word_ref, bins_ref, out_ref, cut_sc):
    tiles, per_block = word_ref.shape
    lane = lax.broadcasted_iota(jnp.int32, (2, LANES), 1)
    at_once = 4

    def take(step, _):
        for u in range(at_once):
            for entry in range(per_block):
                word = word_ref[step * at_once + u, entry]
                row = pl.multiple_of(word >> 7, 2)
                low = bins_ref[pl.ds(row, 2), :]
                high = bins_ref[pl.ds(pl.multiple_of(row + 2, 2), 2), :]
                cut = jnp.where(lane >= (word & (LANES - 1)), low, high)
                at = ((step * at_once + u) * per_block + entry) * 2
                cut_sc[pl.ds(pl.multiple_of(at, 2), 2), :] = pltpu.roll(cut, (-word) & (LANES - 1), 1)
        return 0

    lax.fori_loop(0, tiles // at_once, take, 0)
    out_ref[...] = cut_sc[...].astype(jnp.bfloat16)


def pack(echoes, ids, starts, live):
    pulses, parts, bins = echoes.shape
    panels = bins // LANES
    tiles, per_block = ids.shape
    rows = echoes.astype(jnp.float32).reshape(pulses, parts, panels, LANES).transpose(0, 2, 1, 3)
    rows = jnp.pad(rows, ((0, 0), (1, 1), (0, 0), (0, 0)))
    rows = rows.reshape(pulses * (panels + 2) * parts, LANES)
    offs = starts - lax.axis_index(ROW) * bins
    used = jnp.arange(per_block, dtype=jnp.int32)[None, :] < live
    inside = used & (offs > -LANES) & (offs < bins)
    first = jnp.where(inside, ids * (panels + 2) + (offs >> 7) + 1, panels + 1)
    word = first * (parts * LANES) + (offs & (LANES - 1))
    return pl.pallas_call(
        pack_kernel,
        out_shape=jax.ShapeDtypeStruct((tiles * per_block * parts, LANES), jnp.bfloat16),
        in_specs=[SMEM, VMEM],
        out_specs=VMEM,
        scratch_shapes=[pltpu.VMEM((tiles * per_block * parts, LANES), jnp.float32)],
        compiler_params=pltpu.CompilerParams(vmem_limit_bytes=8 << 20),
        name="pack",
    )(word, rows)


def focus_kernel(got_ref, interp_ref, out_ref):
    tiles = interp_ref.shape[0]
    rows = out_ref.shape[0] // tiles
    panels = got_ref[0].astype(jnp.float32)
    for source in range(1, got_ref.shape[0]):
        panels += got_ref[source].astype(jnp.float32)
    panels = panels.astype(jnp.bfloat16)
    for tile in range(tiles):
        out_ref[tile * rows : (tile + 1) * rows, :] = lax.dot_general(
            panels[tile * rows : (tile + 1) * rows, :],
            interp_ref[tile],
            (((1,), (1,)), ((), ())),
            preferred_element_type=jnp.float32,
        ).astype(jnp.bfloat16)


def focus(got, interp):
    return pl.pallas_call(
        focus_kernel,
        out_shape=jax.ShapeDtypeStruct(got.shape[1:], jnp.bfloat16),
        in_specs=[VMEM] * 2,
        out_specs=VMEM,
        compiler_params=pltpu.CompilerParams(vmem_limit_bytes=4 << 20),
        name="focus",
    )(got, interp)


def place(pair_ref, code_ref, blocks, first, spread):
    tiles = code_ref.shape[0]
    half = spread.shape[0] // 2
    slots = 2 * 32
    wide = code_ref.shape[3]
    side = wide // 2
    row = lax.broadcasted_iota(jnp.int32, (2 * slots, wide), 0)
    for number, ref in enumerate(blocks):
        pair = pair_ref[first + number]
        for tile in range(tiles):
            entries = [ref[(s * tiles + tile) * side : (s * tiles + tile + 1) * side, :] for s in (0, 1)]
            hot = jnp.where(row == code_ref[tile, pair], 1.0, 0.0).astype(jnp.bfloat16)
            placed = jnp.dot(
                hot, jnp.concatenate(entries, 0), preferred_element_type=jnp.float32
            ).astype(jnp.bfloat16)
            columns = slice(tile * LANES, (tile + 1) * LANES)
            spread[number * slots : (number + 1) * slots, columns] = placed[:slots]
            spread[half + number * slots : half + (number + 1) * slots, columns] = placed[slots:]


def turns(coarse_ref, fine_ref, coarse, count, first, pulses):
    columns = pl.ds(first, pulses)
    fine_c, fine_s = fine_ref[0, :, columns], fine_ref[1, :, columns]
    cos, sin = [], []
    for number in range(count):
        here = coarse + number
        coarse_c, coarse_s = coarse_ref[0, here, :, columns], coarse_ref[1, here, :, columns]
        cos.append((coarse_c * fine_c - coarse_s * fine_s).astype(jnp.bfloat16))
        sin.append((-coarse_s * fine_c - coarse_c * fine_s).astype(jnp.bfloat16))
    return jnp.concatenate([jnp.concatenate(cos, 0), jnp.concatenate(sin, 0)], 1)


def part_kernel(pair_ref, code_ref, coarse_ref, fine_ref, *refs, first, n_blocks, more):
    blocks, rest = refs[:n_blocks], refs[n_blocks:]
    held = rest[0] if more else None
    total_ref, spread = rest[-2:]
    place(pair_ref, code_ref, blocks, first, spread)
    count = 4
    rows = count * fine_ref.shape[1]

    def step(number, _):
        here = pl.ds(pl.multiple_of(number * rows, rows), rows)
        left = turns(coarse_ref, fine_ref, number * count, count, first * 64, spread.shape[0] // 2)
        new = jnp.dot(left, spread[...], preferred_element_type=jnp.float32)
        total_ref[here, :] = held[here, :] + new if more else new
        return 0

    lax.fori_loop(0, coarse_ref.shape[1] // count, step, 0)


def last_kernel(pair_ref, code_ref, coarse_ref, fine_ref, *refs, first, n_blocks, scale):
    blocks, (held_ref, out_ref, spread) = refs[:n_blocks], refs[n_blocks:]
    number = pl.program_id(0)

    @pl.when(number == 0)
    def _():
        place(pair_ref, code_ref, blocks, first, spread)

    count = out_ref.shape[0] // FINE_K
    rows = out_ref.shape[0] * 2
    left = turns(coarse_ref, fine_ref, number * count, count, first * 64, spread.shape[0] // 2)
    new = jnp.dot(left, spread[...], preferred_element_type=jnp.float32)
    total = held_ref[pl.ds(pl.multiple_of(number * rows, rows), rows), :] + new
    out_ref[...] = (total * scale).astype(jnp.bfloat16).reshape(out_ref.shape)


def part(pairs, code, coarse, fine, blocks, held, first, scale=None):
    tiles = code.shape[0]
    rows = coarse.shape[1] * fine.shape[1]
    n = tiles * LANES
    depth = len(blocks) * 128
    operands = (pairs, code, coarse, fine, *blocks) + (() if held is None else (held,))
    specs = [SMEM] + [VMEM] * (len(operands) - 1)
    scratch = [pltpu.VMEM((depth, n), jnp.bfloat16)]
    params = pltpu.CompilerParams(vmem_limit_bytes=16 << 20)
    cost = pl.CostEstimate(
        flops=2 * rows * depth * n, transcendentals=0, bytes_accessed=rows * n * 4
    )
    if scale is None:
        return pl.pallas_call(
            functools.partial(
                part_kernel, first=first, n_blocks=len(blocks), more=held is not None
            ),
            out_shape=jax.ShapeDtypeStruct((rows, n), jnp.float32),
            in_specs=specs,
            out_specs=VMEM,
            scratch_shapes=scratch,
            input_output_aliases={} if held is None else {len(operands) - 1: 0},
            compiler_params=params,
            cost_estimate=cost,
            name="part",
        )(*operands)
    step = 128
    return pl.pallas_call(
        functools.partial(last_kernel, first=first, n_blocks=len(blocks), scale=scale),
        out_shape=jax.ShapeDtypeStruct((rows // 2, 2, n), jnp.bfloat16),
        grid=(rows // 2 // step,),
        in_specs=specs,
        out_specs=pl.BlockSpec((step, 2, n), lambda i: (i, 0, 0)),
        scratch_shapes=scratch,
        compiler_params=params,
        cost_estimate=cost,
        name="last",
    )(*operands)


def pick(table, index):
    hot = index[:, None] == jnp.arange(table.shape[0], dtype=jnp.int32)[None, :]
    return jnp.sum(jnp.where(hot[:, :, None], table[None], 0), axis=1)


def twiddles(rates, first_column, columns):
    step_angle = 2.0 * math.pi / COLS
    coarse_k = first_column + FINE_K * jnp.arange(columns // FINE_K, dtype=jnp.int32)
    coarse = ((rates[None, :] * coarse_k[:, None]) % COLS).astype(jnp.float32) * step_angle
    row = jnp.arange(2 * FINE_K, dtype=jnp.int32)
    turn = rates[None, :] * (row // 2)[:, None] + (COLS - (COLS // 4) * (row % 2))[:, None]
    within = (turn % COLS).astype(jnp.float32) * step_angle
    return (
        jnp.stack([jnp.cos(coarse), jnp.sin(coarse)])[:, :, None, :],
        jnp.stack([jnp.cos(within), jnp.sin(within)]),
    )


def body(echoes, pulse_ids, bin_start, live_count, wavenum, interp):
    blocks = lax.axis_size(ANG)
    ang_index = lax.axis_index(ANG)
    n_rows = lax.axis_size(ROW)
    ring = lax.axis_size("z")
    tiles_mine = interp.shape[0]
    block_pulses = echoes.shape[0]
    foot_len = pulse_ids.shape[1]
    per_block = foot_len // blocks
    col_dev = COLS // blocks
    first_entry = ang_index * per_block

    my_ids = lax.dynamic_slice_in_dim(pulse_ids, first_entry, per_block, 1)
    my_starts = lax.dynamic_slice_in_dim(bin_start, first_entry, per_block, 1)
    my_live = lax.dynamic_slice_in_dim(live_count, ang_index, 1, 1)
    packed = pack(echoes, my_ids - ang_index * block_pulses, my_starts, my_live)
    rows = packed.shape[0] // n_rows
    got = lax.all_to_all(packed.reshape(n_rows, rows, LANES), ROW, 0, 0, tiled=True)
    mine = focus(got, interp)

    yh, z, core = (lax.axis_index(name) for name in ANG)
    half = ring // 2
    zs = [0]
    for step in range(1, half + 1):
        zs += [-step] if step == half else [-step, step]
    shift = jnp.repeat(jnp.array(zs, jnp.int32), 2)
    at_core = core ^ (jnp.arange(2 * ring, dtype=jnp.int32) % 2)
    pairs = ((z + shift) % ring) * 2 + at_core
    order = (pairs[:, None] + 2 * ring * (yh ^ jnp.arange(2, dtype=jnp.int32))[None, :]).reshape(-1)
    tile_ids = lax.dynamic_slice_in_dim(
        pulse_ids, lax.axis_index(ROW) * tiles_mine, tiles_mine, 0
    ).reshape(tiles_mine, 2, 2 * ring, per_block)
    tile_ids = jnp.where(yh == 0, tile_ids, tile_ids[:, ::-1]) % block_pulses
    tile_ids = tile_ids + block_pulses * jnp.arange(2, dtype=jnp.int32)[None, :, None, None]
    code = tile_ids.transpose(0, 2, 1, 3)[..., None] + 2 * block_pulses * jnp.arange(2, dtype=jnp.int32)
    code = code.reshape(tiles_mine, 2 * ring, 1, 4 * per_block)
    rates = pick(wavenum.reshape(blocks, block_pulses), order).reshape(-1)
    coarse, fine = twiddles(rates, ang_index * col_dev, col_dev)

    swap = [(0, 1), (1, 0)]
    ahead = [(i, (i + 1) % ring) for i in range(ring)]
    behind = [(i, (i - 1) % ring) for i in range(ring)]
    other = lax.ppermute(mine, "yh", swap)
    forward = backward = jnp.concatenate([mine, other], 0)
    held = [forward]
    for step in range(1, half + 1):
        forward = lax.ppermute(forward, "z", ahead)
        held.append(forward)
        if step < half:
            backward = lax.ppermute(backward, "z", behind)
            held.append(backward)
    arrays = []
    for near in held:
        arrays += [near, lax.ppermute(near, "core", swap)]
    total = None
    cuts = [0, 6, 10, 14, 16]
    for first, last in zip(cuts, cuts[1:]):
        scale = foot_len ** (-0.5) if last == len(arrays) else None
        total = part(pairs, code, coarse, fine, arrays[first:last], total, first, scale)
    return total


def solution(mesh):
    finer = Mesh(mesh.devices.reshape(2, -1, 2, 4, 2), FINE)
    return jax.shard_map(
        body,
        mesh=finer,
        in_specs=(P(ANG, None, ROW), P(), P(), P(), P(), P(ROW, None, None)),
        out_specs=P(ANG, None, ROW),
        check_vma=False,
    )
```

```python
import functools
import math

import jax
import jax.numpy as jnp
from jax import lax
from jax.experimental import pallas as pl
from jax.experimental.pallas import tpu as pltpu
from jax.sharding import Mesh
from jax.sharding import PartitionSpec as P

COLS = 32768
LANES = 128
FINE_K = 32
ANG = ("yh", "z", "core")
ROW = ("x", "yl")
FINE = ("yh", "z", "core", "x", "yl")
SMEM = pl.BlockSpec(memory_space=pltpu.SMEM)
VMEM = pl.BlockSpec(memory_space=pltpu.VMEM)


def pack_kernel(word_ref, bins_ref, out_ref, cut_sc):
    tiles, per_block = word_ref.shape
    lane = lax.broadcasted_iota(jnp.int32, (2, LANES), 1)
    at_once = 4

    def take(step, _):
        for u in range(at_once):
            for entry in range(per_block):
                word = word_ref[step * at_once + u, entry]
                row = pl.multiple_of(word >> 7, 2)
                low = bins_ref[pl.ds(row, 2), :]
                high = bins_ref[pl.ds(pl.multiple_of(row + 2, 2), 2), :]
                cut = jnp.where(lane >= (word & (LANES - 1)), low, high)
                at = ((step * at_once + u) * per_block + entry) * 2
                cut_sc[pl.ds(pl.multiple_of(at, 2), 2), :] = pltpu.roll(cut, (-word) & (LANES - 1), 1)
        return 0

    lax.fori_loop(0, tiles // at_once, take, 0)
    out_ref[...] = cut_sc[...].astype(jnp.bfloat16)


def pack(echoes, ids, starts, live):
    pulses, parts, bins = echoes.shape
    panels = bins // LANES
    tiles, per_block = ids.shape
    rows = echoes.astype(jnp.float32).reshape(pulses, parts, panels, LANES).transpose(0, 2, 1, 3)
    rows = jnp.pad(rows, ((0, 0), (1, 1), (0, 0), (0, 0)))
    rows = rows.reshape(pulses * (panels + 2) * parts, LANES)
    offs = starts - lax.axis_index(ROW) * bins
    used = jnp.arange(per_block, dtype=jnp.int32)[None, :] < live
    inside = used & (offs > -LANES) & (offs < bins)
    first = jnp.where(inside, ids * (panels + 2) + (offs >> 7) + 1, panels + 1)
    word = first * (parts * LANES) + (offs & (LANES - 1))
    return pl.pallas_call(
        pack_kernel,
        out_shape=jax.ShapeDtypeStruct((tiles * per_block * parts, LANES), jnp.bfloat16),
        in_specs=[SMEM, VMEM],
        out_specs=VMEM,
        scratch_shapes=[pltpu.VMEM((tiles * per_block * parts, LANES), jnp.float32)],
        compiler_params=pltpu.CompilerParams(vmem_limit_bytes=8 << 20),
        name="pack",
    )(word, rows)


def focus_kernel(got_ref, turned_ref, out_ref):
    tiles = turned_ref.shape[0]
    rows = out_ref.shape[0] // tiles
    panels = got_ref[0].astype(jnp.float32)
    for source in range(1, got_ref.shape[0]):
        panels += got_ref[source].astype(jnp.float32)
    panels = panels.astype(jnp.bfloat16)
    for tile in range(tiles):
        out_ref[tile * rows : (tile + 1) * rows, :] = lax.dot_general(
            panels[tile * rows : (tile + 1) * rows, :],
            turned_ref[tile],
            (((1,), (0,)), ((), ())),
            preferred_element_type=jnp.float32,
        ).astype(jnp.bfloat16)


def focus(got, turned):
    return pl.pallas_call(
        focus_kernel,
        out_shape=jax.ShapeDtypeStruct(got.shape[1:], jnp.bfloat16),
        in_specs=[VMEM] * 2,
        out_specs=VMEM,
        compiler_params=pltpu.CompilerParams(vmem_limit_bytes=4 << 20),
        name="focus",
    )(got, turned)


def place(pair_ref, code_ref, blocks, first, spread):
    tiles = code_ref.shape[0]
    half = spread.shape[0] // 2
    slots = 2 * 32
    wide = code_ref.shape[3]
    side = wide // 2
    row = lax.broadcasted_iota(jnp.int32, (2 * slots, wide), 0)
    for number, ref in enumerate(blocks):
        pair = pair_ref[first + number]
        for tile in range(tiles):
            entries = [ref[(s * tiles + tile) * side : (s * tiles + tile + 1) * side, :] for s in (0, 1)]
            hot = jnp.where(row == code_ref[tile, pair], 1.0, 0.0).astype(jnp.bfloat16)
            placed = jnp.dot(
                hot, jnp.concatenate(entries, 0), preferred_element_type=jnp.float32
            ).astype(jnp.bfloat16)
            columns = slice(tile * LANES, (tile + 1) * LANES)
            spread[number * slots : (number + 1) * slots, columns] = placed[:slots]
            spread[half + number * slots : half + (number + 1) * slots, columns] = placed[slots:]


def turn_kernel(coarse_ref, fine_ref, *out_refs):
    pulses = coarse_ref.shape[3] // len(out_refs)
    rows = fine_ref.shape[1]

    def step(number, _):
        here = pl.ds(pl.multiple_of(number * rows, rows), rows)
        for which, out_ref in enumerate(out_refs):
            columns = pl.ds(which * pulses, pulses)
            coarse_c, coarse_s = coarse_ref[0, number, :, columns], coarse_ref[1, number, :, columns]
            fine_c, fine_s = fine_ref[0, :, columns], fine_ref[1, :, columns]
            out_ref[here, :pulses] = (coarse_c * fine_c - coarse_s * fine_s).astype(jnp.bfloat16)
            out_ref[here, pulses:] = (-coarse_s * fine_c - coarse_c * fine_s).astype(jnp.bfloat16)
        return 0

    lax.fori_loop(0, coarse_ref.shape[1], step, 0, unroll=4)


def turns(coarse, fine, parts):
    rows = coarse.shape[1] * fine.shape[1]
    shape = jax.ShapeDtypeStruct((rows, 2 * coarse.shape[3] // parts), jnp.bfloat16)
    return pl.pallas_call(
        turn_kernel,
        out_shape=[shape] * parts,
        in_specs=[VMEM] * 2,
        out_specs=[VMEM] * parts,
        compiler_params=pltpu.CompilerParams(vmem_limit_bytes=24 << 20),
        name="turns",
    )(coarse, fine)


def part_kernel(pair_ref, code_ref, turn_ref, *refs, first, n_blocks, more):
    blocks, rest = refs[:n_blocks], refs[n_blocks:]
    total_ref, spread = rest[-2:]
    place(pair_ref, code_ref, blocks, first, spread)
    rows = 512
    for start in range(0, turn_ref.shape[0], rows):
        here = slice(start, start + rows)
        new = jnp.dot(turn_ref[here, :], spread[...], preferred_element_type=jnp.float32)
        total_ref[here, :] = rest[0][here, :] + new if more else new


def last_kernel(pair_ref, code_ref, turn_ref, *refs, first, n_blocks, scale):
    blocks, (held_ref, out_ref, spread, ready, sems) = refs[:n_blocks], refs[n_blocks:]
    place(pair_ref, code_ref, blocks, first, spread)
    copies = sems.shape[0]
    columns = ready.shape[0] // copies
    rows = 2 * columns
    sent = []
    for number in range(copies):
        here = slice(number * rows, (number + 1) * rows)
        new = jnp.dot(turn_ref[here, :], spread[...], preferred_element_type=jnp.float32)
        total = ((held_ref[here, :] + new) * scale).astype(jnp.bfloat16)
        there = pl.ds(number * columns, columns)
        ready[there] = total.reshape((columns,) + ready.shape[1:])
        copy = pltpu.make_async_copy(ready.at[there], out_ref.at[there], sems.at[number])
        copy.start()
        sent.append(copy)
    for copy in sent:
        copy.wait()


def part(pairs, code, turn, blocks, held, first, scale=None):
    tiles = code.shape[0]
    rows, depth = turn.shape
    n = tiles * LANES
    operands = (pairs, code, turn, *blocks) + (() if held is None else (held,))
    specs = [SMEM] + [VMEM] * (len(operands) - 1)
    scratch = [pltpu.VMEM((depth, n), jnp.bfloat16)]
    params = pltpu.CompilerParams(vmem_limit_bytes=24 << 20)
    if scale is None:
        return pl.pallas_call(
            functools.partial(
                part_kernel, first=first, n_blocks=len(blocks), more=held is not None
            ),
            out_shape=jax.ShapeDtypeStruct((rows, n), jnp.float32),
            in_specs=specs,
            out_specs=VMEM,
            scratch_shapes=scratch,
            input_output_aliases={} if held is None else {len(operands) - 1: 0},
            compiler_params=params,
            name="part",
        )(*operands)
    shape = jax.ShapeDtypeStruct((rows // 2, 2, n), jnp.bfloat16)
    return pl.pallas_call(
        functools.partial(last_kernel, first=first, n_blocks=len(blocks), scale=scale),
        out_shape=shape,
        in_specs=specs,
        out_specs=pl.BlockSpec(memory_space=pl.ANY),
        scratch_shapes=scratch
        + [pltpu.VMEM(shape.shape, shape.dtype), pltpu.SemaphoreType.DMA((8,))],
        compiler_params=params,
        name="last",
    )(*operands)


def pick(table, index):
    hot = index[:, None] == jnp.arange(table.shape[0], dtype=jnp.int32)[None, :]
    return jnp.sum(jnp.where(hot[:, :, None], table[None], 0), axis=1)


def twiddles(rates, first_column, columns):
    step_angle = 2.0 * math.pi / COLS
    coarse_k = first_column + FINE_K * jnp.arange(columns // FINE_K, dtype=jnp.int32)
    coarse = ((rates[None, :] * coarse_k[:, None]) % COLS).astype(jnp.float32) * step_angle
    row = jnp.arange(2 * FINE_K, dtype=jnp.int32)
    turn = rates[None, :] * (row // 2)[:, None] + (COLS - (COLS // 4) * (row % 2))[:, None]
    within = (turn % COLS).astype(jnp.float32) * step_angle
    return (
        jnp.stack([jnp.cos(coarse), jnp.sin(coarse)])[:, :, None, :],
        jnp.stack([jnp.cos(within), jnp.sin(within)]),
    )


def body(echoes, pulse_ids, bin_start, live_count, wavenum, interp):
    blocks = lax.axis_size(ANG)
    ang_index = lax.axis_index(ANG)
    n_rows = lax.axis_size(ROW)
    ring = lax.axis_size("z")
    tiles_mine = interp.shape[0]
    block_pulses = echoes.shape[0]
    foot_len = pulse_ids.shape[1]
    per_block = foot_len // blocks
    col_dev = COLS // blocks
    first_entry = ang_index * per_block

    my_ids = lax.dynamic_slice_in_dim(pulse_ids, first_entry, per_block, 1)
    my_starts = lax.dynamic_slice_in_dim(bin_start, first_entry, per_block, 1)
    my_live = lax.dynamic_slice_in_dim(live_count, ang_index, 1, 1)
    packed = pack(echoes, my_ids - ang_index * block_pulses, my_starts, my_live)
    rows = packed.shape[0] // n_rows
    got = lax.all_to_all(packed.reshape(n_rows, rows, LANES), ROW, 0, 0, tiled=True)
    mine = focus(got, interp.swapaxes(1, 2))

    yh, z, core = (lax.axis_index(name) for name in ANG)
    half = ring // 2
    shift, side = [0, 0, -1, 1], [0, 1, 0, 0]
    for step in range(2, half):
        shift += [1 - step, step - 1, -step, step]
        side += [1, 1, 0, 0]
    shift = jnp.array(shift + [1 - half, half - 1, half, half], jnp.int32)
    side = jnp.array(side + [1, 1, 0, 1], jnp.int32)
    pairs = ((z + shift) % ring) * 2 + (core ^ side)
    order = (pairs[:, None] + 2 * ring * (yh ^ jnp.arange(2, dtype=jnp.int32))[None, :]).reshape(-1)
    tile_ids = lax.dynamic_slice_in_dim(
        pulse_ids, lax.axis_index(ROW) * tiles_mine, tiles_mine, 0
    ).reshape(tiles_mine, 2, 2 * ring, per_block)
    tile_ids = jnp.where(yh == 0, tile_ids, tile_ids[:, ::-1]) % block_pulses
    tile_ids = tile_ids + block_pulses * jnp.arange(2, dtype=jnp.int32)[None, :, None, None]
    code = tile_ids.transpose(0, 2, 1, 3)[..., None] + 2 * block_pulses * jnp.arange(2, dtype=jnp.int32)
    code = code.reshape(tiles_mine, 2 * ring, 1, 4 * per_block)
    rates = pick(wavenum.reshape(blocks, block_pulses), order).reshape(-1)
    coarse, fine = twiddles(rates, ang_index * col_dev, col_dev)

    tables = turns(coarse, fine, half)

    swap = [(0, 1), (1, 0)]
    ahead = [(i, (i + 1) % ring) for i in range(ring)]
    behind = [(i, (i - 1) % ring) for i in range(ring)]
    other = lax.ppermute(mine, "yh", swap)
    forward = backward = jnp.concatenate([mine, other], 0)
    near = [forward]
    far, total = [], None
    for step in range(1, half):
        arriving = lax.ppermute(forward, "z", ahead), lax.ppermute(backward, "z", behind)
        far = [lax.ppermute(block, "core", swap) for block in near]
        if step > 1:
            total = part(pairs, code, tables[step - 2], blocks, total, 4 * (step - 2))
            forward, backward, total = lax.optimization_barrier((*arriving, total))
        else:
            forward, backward = lax.optimization_barrier(arriving)
        blocks = ([*near] if step == 1 else []) + far + [forward, backward]
        near = [forward, backward]
    opposite = lax.ppermute(forward, "z", ahead)
    far = [lax.ppermute(block, "core", swap) for block in near]
    total = part(pairs, code, tables[half - 2], blocks, total, 4 * (half - 2))
    opposite, total = lax.optimization_barrier((opposite, total))
    blocks = far + [opposite, lax.ppermute(opposite, "core", swap)]
    return part(pairs, code, tables[half - 1], blocks, total, 4 * (half - 1), foot_len ** (-0.5))


def solution(mesh):
    finer = Mesh(mesh.devices.reshape(2, -1, 2, 4, 2), FINE)
    return jax.shard_map(
        body,
        mesh=finer,
        in_specs=(P(ANG, None, ROW), P(), P(), P(), P(), P(ROW, None, None)),
        out_specs=P(ANG, None, ROW),
        check_vma=False,
    )
```

```python
import functools
import math

import jax
import jax.numpy as jnp
from jax import lax
from jax.experimental import pallas as pl
from jax.experimental.pallas import tpu as pltpu
from jax.sharding import Mesh
from jax.sharding import PartitionSpec as P

COLS = 32768
LANES = 128
FINE_K = 32
ANG = ("yh", "z", "core")
ROW = ("x", "yl")
FINE = ("yh", "z", "core", "x", "yl")
SMEM = pl.BlockSpec(memory_space=pltpu.SMEM)
VMEM = pl.BlockSpec(memory_space=pltpu.VMEM)

def pack_kernel(word_ref, bins_ref, out_ref, cut_sc):
    tiles, per_block = word_ref.shape
    lane = lax.broadcasted_iota(jnp.int32, (2, LANES), 1)
    at_once = 4

    def take(step, _):
        for u in range(at_once):
            for entry in range(per_block):
                word = word_ref[step * at_once + u, entry]
                row = pl.multiple_of(word >> 7, 2)
                low = bins_ref[pl.ds(row, 2), :]
                high = bins_ref[pl.ds(pl.multiple_of(row + 2, 2), 2), :]
                at = ((step * at_once + u) * per_block + entry) * 2
                cut_sc[pl.ds(pl.multiple_of(at, 2), 2), :] = jnp.where(
                    lane >= (word & (LANES - 1)), low, high
                )
        return 0

    lax.fori_loop(0, tiles // at_once, take, 0)
    out_ref[...] = cut_sc[...].astype(jnp.bfloat16)

def pack(echoes, ids, starts, live):
    pulses, parts, bins = echoes.shape
    panels = bins // LANES
    tiles, per_block = ids.shape
    rows = echoes.astype(jnp.float32).reshape(pulses, parts, panels, LANES).transpose(0, 2, 1, 3)
    rows = jnp.pad(rows, ((0, 0), (1, 1), (0, 0), (0, 0)))
    rows = rows.reshape(pulses * (panels + 2) * parts, LANES)
    offs = starts - lax.axis_index(ROW) * bins
    used = jnp.arange(per_block, dtype=jnp.int32)[None, :] < live
    inside = used & (offs > -LANES) & (offs < bins)
    first = jnp.where(inside, ids * (panels + 2) + (offs >> 7) + 1, panels + 1)
    word = first * (parts * LANES) + (offs & (LANES - 1))
    return pl.pallas_call(
        pack_kernel,
        out_shape=jax.ShapeDtypeStruct((tiles * per_block * parts, LANES), jnp.bfloat16),
        in_specs=[SMEM, VMEM],
        out_specs=VMEM,
        scratch_shapes=[pltpu.VMEM((tiles * per_block * parts, LANES), jnp.float32)],
        compiler_params=pltpu.CompilerParams(vmem_limit_bytes=8 << 20),
        name="pack",
    )(word, rows)

def focus_kernel(back_ref, got_ref, turned_ref, out_ref, panels):
    tiles, per_block = back_ref.shape
    rows = out_ref.shape[0] // tiles
    total = got_ref[0].astype(jnp.float32)
    for source in range(1, got_ref.shape[0]):
        total += got_ref[source].astype(jnp.float32)
    panels[...] = total
    for tile in range(tiles):
        windows = []
        for entry in range(per_block):
            at = tile * rows + entry * 2
            windows.append(pltpu.roll(panels[at : at + 2, :], back_ref[tile, entry], 1))
        out_ref[tile * rows : (tile + 1) * rows, :] = jnp.dot(
            jnp.concatenate(windows, 0).astype(jnp.bfloat16),
            turned_ref[tile],
            preferred_element_type=jnp.float32,
        ).astype(jnp.bfloat16)


def focus(back, got, turned):
    return pl.pallas_call(
        focus_kernel,
        out_shape=jax.ShapeDtypeStruct(got.shape[1:], jnp.bfloat16),
        in_specs=[SMEM, VMEM, VMEM],
        out_specs=VMEM,
        scratch_shapes=[pltpu.VMEM(got.shape[1:], jnp.float32)],
        compiler_params=pltpu.CompilerParams(vmem_limit_bytes=4 << 20),
        name="focus",
    )(back, got, turned)


def place(pair_ref, code_ref, blocks, first, spread):
    tiles = code_ref.shape[0]
    half = spread.shape[0] // 2
    slots = 2 * 32
    wide = code_ref.shape[3]
    side = wide // 2
    row = lax.broadcasted_iota(jnp.int32, (2 * slots, wide), 0)
    for number, ref in enumerate(blocks):
        pair = pair_ref[first + number]
        for tile in range(tiles):
            entries = [ref[(s * tiles + tile) * side : (s * tiles + tile + 1) * side, :] for s in (0, 1)]
            hot = jnp.where(row == code_ref[tile, pair], 1.0, 0.0).astype(jnp.bfloat16)
            placed = jnp.dot(
                hot, jnp.concatenate(entries, 0), preferred_element_type=jnp.float32
            ).astype(jnp.bfloat16)
            columns = slice(tile * LANES, (tile + 1) * LANES)
            spread[number * slots : (number + 1) * slots, columns] = placed[:slots]
            spread[half + number * slots : half + (number + 1) * slots, columns] = placed[slots:]

def turn_kernel(coarse_ref, fine_ref, *out_refs):
    pulses = coarse_ref.shape[3] // len(out_refs)
    rows = fine_ref.shape[1]

    def step(number, _):
        here = pl.ds(pl.multiple_of(number * rows, rows), rows)
        for which, out_ref in enumerate(out_refs):
            columns = pl.ds(which * pulses, pulses)
            coarse_c, coarse_s = coarse_ref[0, number, :, columns], coarse_ref[1, number, :, columns]
            fine_c, fine_s = fine_ref[0, :, columns], fine_ref[1, :, columns]
            out_ref[here, :pulses] = (coarse_c * fine_c - coarse_s * fine_s).astype(jnp.bfloat16)
            out_ref[here, pulses:] = (-coarse_s * fine_c - coarse_c * fine_s).astype(jnp.bfloat16)
        return 0

    lax.fori_loop(0, coarse_ref.shape[1], step, 0, unroll=4)

def turns(coarse, fine, parts):
    rows = coarse.shape[1] * fine.shape[1]
    shape = jax.ShapeDtypeStruct((rows, 2 * coarse.shape[3] // parts), jnp.bfloat16)
    return pl.pallas_call(
        turn_kernel,
        out_shape=[shape] * parts,
        in_specs=[VMEM] * 2,
        out_specs=[VMEM] * parts,
        compiler_params=pltpu.CompilerParams(vmem_limit_bytes=2 << 20),
        name="turns",
    )(coarse, fine)

def part_kernel(pair_ref, code_ref, turn_ref, *refs, first, n_blocks, more):
    blocks, rest = refs[:n_blocks], refs[n_blocks:]
    total_ref, spread = rest[-2:]
    place(pair_ref, code_ref, blocks, first, spread)
    rows = 512
    for start in range(0, turn_ref.shape[0], rows):
        here = slice(start, start + rows)
        new = jnp.dot(turn_ref[here, :], spread[...], preferred_element_type=jnp.float32)
        total_ref[here, :] = rest[0][here, :] + new if more else new

def last_kernel(pair_ref, code_ref, turn_ref, *refs, first, n_blocks, scale):
    blocks, (held_ref, out_ref, spread, ready, sems) = refs[:n_blocks], refs[n_blocks:]
    place(pair_ref, code_ref, blocks, first, spread)
    copies = sems.shape[0]
    columns = ready.shape[0] // copies
    rows = 2 * columns
    sent = []
    for number in range(copies):
        here = slice(number * rows, (number + 1) * rows)
        new = jnp.dot(turn_ref[here, :], spread[...], preferred_element_type=jnp.float32)
        total = ((held_ref[here, :] + new) * scale).astype(jnp.bfloat16)
        there = pl.ds(number * columns, columns)
        ready[there] = total.reshape((columns,) + ready.shape[1:])
        copy = pltpu.make_async_copy(ready.at[there], out_ref.at[there], sems.at[number])
        copy.start()
        sent.append(copy)
    for copy in sent:
        copy.wait()

def part(pairs, code, turn, blocks, held, first, scale=None):
    tiles = code.shape[0]
    rows, depth = turn.shape
    n = tiles * LANES
    operands = (pairs, code, turn, *blocks) + (() if held is None else (held,))
    specs = [SMEM] + [VMEM] * (len(operands) - 1)
    scratch = [pltpu.VMEM((depth, n), jnp.bfloat16)]
    params = pltpu.CompilerParams(vmem_limit_bytes=(6 if scale is None else 10) << 20)
    if scale is None:
        return pl.pallas_call(
            functools.partial(
                part_kernel, first=first, n_blocks=len(blocks), more=held is not None
            ),
            out_shape=jax.ShapeDtypeStruct((rows, n), jnp.float32),
            in_specs=specs,
            out_specs=VMEM,
            scratch_shapes=scratch,
            input_output_aliases={} if held is None else {len(operands) - 1: 0},
            compiler_params=params,
            name="part",
        )(*operands)
    shape = jax.ShapeDtypeStruct((rows // 2, 2, n), jnp.bfloat16)
    return pl.pallas_call(
        functools.partial(last_kernel, first=first, n_blocks=len(blocks), scale=scale),
        out_shape=shape,
        in_specs=specs,
        out_specs=pl.BlockSpec(memory_space=pl.ANY),
        scratch_shapes=scratch
        + [pltpu.VMEM(shape.shape, shape.dtype), pltpu.SemaphoreType.DMA((8,))],
        compiler_params=params,
        name="last",
    )(*operands)

def pick(table, index):
    hot = index[:, None] == jnp.arange(table.shape[0], dtype=jnp.int32)[None, :]
    return jnp.sum(jnp.where(hot[:, :, None], table[None], 0), axis=1)

def twiddles(rates, first_column, columns):
    step_angle = 2.0 * math.pi / COLS
    coarse_k = first_column + FINE_K * jnp.arange(columns // FINE_K, dtype=jnp.int32)
    coarse = ((rates[None, :] * coarse_k[:, None]) % COLS).astype(jnp.float32) * step_angle
    row = jnp.arange(2 * FINE_K, dtype=jnp.int32)
    turn = rates[None, :] * (row // 2)[:, None] + (COLS - (COLS // 4) * (row % 2))[:, None]
    within = (turn % COLS).astype(jnp.float32) * step_angle
    return (
        jnp.stack([jnp.cos(coarse), jnp.sin(coarse)])[:, :, None, :],
        jnp.stack([jnp.cos(within), jnp.sin(within)]),
    )

def body(echoes, pulse_ids, bin_start, live_count, wavenum, interp):
    blocks = lax.axis_size(ANG)
    ang_index = lax.axis_index(ANG)
    n_rows = lax.axis_size(ROW)
    ring = lax.axis_size("z")
    tiles_mine = interp.shape[0]
    block_pulses = echoes.shape[0]
    foot_len = pulse_ids.shape[1]
    per_block = foot_len // blocks
    col_dev = COLS // blocks
    first_entry = ang_index * per_block

    my_ids = lax.dynamic_slice_in_dim(pulse_ids, first_entry, per_block, 1)
    my_starts = lax.dynamic_slice_in_dim(bin_start, first_entry, per_block, 1)
    my_live = lax.dynamic_slice_in_dim(live_count, ang_index, 1, 1)
    packed = pack(echoes, my_ids - ang_index * block_pulses, my_starts, my_live)
    rows = packed.shape[0] // n_rows
    got = lax.all_to_all(packed.reshape(n_rows, rows, LANES), ROW, 0, 0, tiled=True)
    my_tiles = lax.axis_index(ROW) * tiles_mine
    back = (-lax.dynamic_slice(bin_start, (my_tiles, first_entry), (tiles_mine, per_block))) & (LANES - 1)
    mine = focus(back, got, interp.swapaxes(1, 2))

    yh, z, core = (lax.axis_index(name) for name in ANG)
    half = ring // 2
    shift, side = [0, 0, -1, 1], [0, 1, 0, 0]
    for step in range(2, half):
        shift += [1 - step, step - 1, -step, step]
        side += [1, 1, 0, 0]
    shift = jnp.array(shift + [1 - half, half - 1, half, half], jnp.int32)
    side = jnp.array(side + [1, 1, 0, 1], jnp.int32)
    pairs = ((z + shift) % ring) * 2 + (core ^ side)
    order = (pairs[:, None] + 2 * ring * (yh ^ jnp.arange(2, dtype=jnp.int32))[None, :]).reshape(-1)
    tile_ids = lax.dynamic_slice_in_dim(
        pulse_ids, my_tiles, tiles_mine, 0
    ).reshape(tiles_mine, 2, 2 * ring, per_block)
    tile_ids = jnp.where(yh == 0, tile_ids, tile_ids[:, ::-1]) % block_pulses
    tile_ids = tile_ids + block_pulses * jnp.arange(2, dtype=jnp.int32)[None, :, None, None]
    code = tile_ids.transpose(0, 2, 1, 3)[..., None] + 2 * block_pulses * jnp.arange(2, dtype=jnp.int32)
    code = code.reshape(tiles_mine, 2 * ring, 1, 4 * per_block)
    rates = pick(wavenum.reshape(blocks, block_pulses), order).reshape(-1)
    coarse, fine = twiddles(rates, ang_index * col_dev, col_dev)

    tables = turns(coarse, fine, half)

    swap = [(0, 1), (1, 0)]
    ahead = [(i, (i + 1) % ring) for i in range(ring)]
    behind = [(i, (i - 1) % ring) for i in range(ring)]
    other = lax.ppermute(mine, "yh", swap)

    forward = backward = jnp.concatenate([mine, other], 0)
    near = [forward]
    far, total = [], None
    for step in range(1, half):
        arriving = lax.ppermute(forward, "z", ahead), lax.ppermute(backward, "z", behind)
        if step > 1:
            total = part(pairs, code, tables[step - 2], blocks, total, 4 * (step - 2))
            *leaving, total = lax.optimization_barrier((*near, total))
            far = [lax.ppermute(block, "core", swap) for block in leaving]
            forward, backward, total = lax.optimization_barrier((*arriving, total))
        else:
            far = [lax.ppermute(block, "core", swap) for block in near]
            forward, backward = lax.optimization_barrier(arriving)
        blocks = ([*near] if step == 1 else []) + far + [forward, backward]
        near = [forward, backward]
    opposite = lax.ppermute(forward, "z", ahead)
    far = [lax.ppermute(block, "core", swap) for block in near]
    total = part(pairs, code, tables[half - 2], blocks, total, 4 * (half - 2))
    opposite, total = lax.optimization_barrier((opposite, total))
    blocks = far + [opposite, lax.ppermute(opposite, "core", swap)]
    return part(pairs, code, tables[half - 1], blocks, total, 4 * (half - 1), foot_len ** (-0.5))

def solution(mesh):
    finer = Mesh(mesh.devices.reshape(2, -1, 2, 4, 2), FINE)
    return jax.shard_map(
        body,
        mesh=finer,
        in_specs=(P(ANG, None, ROW), P(), P(), P(), P(), P(ROW, None, None)),
        out_specs=P(ANG, None, ROW),
        check_vma=False,
    )
```

```python
import functools
import math

import jax
import jax.numpy as jnp
from jax import lax
from jax.experimental import pallas as pl
from jax.experimental.pallas import tpu as pltpu
from jax.sharding import Mesh
from jax.sharding import PartitionSpec as P

COLS = 32768
LANES = 128
FINE_K = 32
ANG = ("yh", "z", "core")
ROW = ("x", "yl")
FINE = ("yh", "z", "core", "x", "yl")
SMEM = pl.BlockSpec(memory_space=pltpu.SMEM)
VMEM = pl.BlockSpec(memory_space=pltpu.VMEM)

def pack_kernel(word_ref, bins_ref, out_ref):
    tiles, per_block = word_ref.shape
    _, parts, lanes = bins_ref.shape
    lane = lax.broadcasted_iota(jnp.int32, (parts, lanes), 1)
    at_once = 4

    def take(step, _):
        for u in range(at_once):
            for entry in range(per_block):
                word = word_ref[step * at_once + u, entry]
                row = word >> 7
                low = bins_ref[row].astype(jnp.float32)
                high = bins_ref[row + 1].astype(jnp.float32)
                cut = jnp.where(lane >= (word & (lanes - 1)), low, high)
                out_ref[(step * at_once + u) * per_block + entry] = cut.astype(out_ref.dtype)
        return 0

    lax.fori_loop(0, tiles // at_once, take, 0)


def pack(echoes, ids, starts, live):
    pulses, parts, bins = echoes.shape
    panels = bins // LANES
    tiles, per_block = ids.shape
    rows = echoes.reshape(pulses, parts, panels, LANES).transpose(0, 2, 1, 3)
    rows = jnp.pad(rows, ((0, 0), (1, 1), (0, 0), (0, 0)))
    offs = starts - lax.axis_index(ROW) * bins
    used = jnp.arange(per_block, dtype=jnp.int32)[None, :] < live
    inside = used & (offs > -LANES) & (offs < bins)
    first = jnp.where(inside, ids * (panels + 2) + (offs >> 7) + 1, panels + 1)
    word = first * LANES + (offs & (LANES - 1))
    return pl.pallas_call(
        pack_kernel,
        out_shape=jax.ShapeDtypeStruct((tiles * per_block, parts, LANES), echoes.dtype),
        in_specs=[SMEM, VMEM],
        out_specs=VMEM,
        compiler_params=pltpu.CompilerParams(vmem_limit_bytes=4 << 20),
        name="pack",
    )(word, rows.reshape(pulses * (panels + 2), parts, LANES))


def focus_kernel(back_ref, got_ref, turned_ref, out_ref, panels):
    tiles, per_block = back_ref.shape
    rows = out_ref.shape[0] // tiles
    total = got_ref[0].astype(jnp.float32)
    for source in range(1, got_ref.shape[0]):
        total += got_ref[source].astype(jnp.float32)
    panels[...] = total
    for tile in range(tiles):
        windows = []
        for entry in range(per_block):
            at = tile * rows + entry * 2
            windows.append(pltpu.roll(panels[at : at + 2, :], back_ref[tile, entry], 1))
        out_ref[tile * rows : (tile + 1) * rows, :] = jnp.dot(
            jnp.concatenate(windows, 0).astype(jnp.bfloat16),
            turned_ref[tile],
            preferred_element_type=jnp.float32,
        ).astype(jnp.bfloat16)


def focus(back, got, turned):
    return pl.pallas_call(
        focus_kernel,
        out_shape=jax.ShapeDtypeStruct(got.shape[1:], jnp.bfloat16),
        in_specs=[SMEM, VMEM, VMEM],
        out_specs=VMEM,
        scratch_shapes=[pltpu.VMEM(got.shape[1:], jnp.float32)],
        compiler_params=pltpu.CompilerParams(vmem_limit_bytes=4 << 20),
        name="focus",
    )(back, got, turned)


def place(pair_ref, code_ref, blocks, first, spread):
    tiles = code_ref.shape[0]
    half = spread.shape[0] // 2
    slots = 2 * 32
    wide = code_ref.shape[3]
    side = wide // 2
    row = lax.broadcasted_iota(jnp.int32, (2 * slots, wide), 0)
    for number, ref in enumerate(blocks):
        pair = pair_ref[first + number]
        for tile in range(tiles):
            entries = [ref[(s * tiles + tile) * side : (s * tiles + tile + 1) * side, :] for s in (0, 1)]
            hot = jnp.where(row == code_ref[tile, pair], 1.0, 0.0).astype(jnp.bfloat16)
            placed = jnp.dot(
                hot, jnp.concatenate(entries, 0), preferred_element_type=jnp.float32
            ).astype(jnp.bfloat16)
            columns = slice(tile * LANES, (tile + 1) * LANES)
            spread[number * slots : (number + 1) * slots, columns] = placed[:slots]
            spread[half + number * slots : half + (number + 1) * slots, columns] = placed[slots:]

def turn_kernel(coarse_ref, fine_ref, mark_ref, *out_refs):
    pulses = coarse_ref.shape[3] // len(out_refs)
    rows = fine_ref.shape[1]

    def step(number, _):
        here = pl.ds(pl.multiple_of(number * rows, rows), rows)
        for which, out_ref in enumerate(out_refs):
            columns = pl.ds(which * pulses, pulses)
            coarse_c, coarse_s = coarse_ref[0, number, :, columns], coarse_ref[1, number, :, columns]
            fine_c, fine_s = fine_ref[0, :, columns], fine_ref[1, :, columns]
            out_ref[here, :pulses] = (coarse_c * fine_c - coarse_s * fine_s).astype(jnp.bfloat16)
            out_ref[here, pulses:] = (-coarse_s * fine_c - coarse_c * fine_s).astype(jnp.bfloat16)
        return 0

    lax.fori_loop(0, coarse_ref.shape[1], step, 0, unroll=4)
    mark_ref[...] = jnp.zeros(mark_ref.shape, mark_ref.dtype)

def turns(coarse, fine, parts):
    rows = coarse.shape[1] * fine.shape[1]
    shape = jax.ShapeDtypeStruct((rows, 2 * coarse.shape[3] // parts), jnp.bfloat16)
    return pl.pallas_call(
        turn_kernel,
        out_shape=[jax.ShapeDtypeStruct((8, LANES), jnp.float32)] + [shape] * parts,
        in_specs=[VMEM] * 2,
        out_specs=[VMEM] * (parts + 1),
        compiler_params=pltpu.CompilerParams(vmem_limit_bytes=2 << 20),
        name="turns",
    )(coarse, fine)

def part_kernel(pair_ref, code_ref, turn_ref, *refs, first, n_blocks, more):
    blocks, rest = refs[:n_blocks], refs[n_blocks:]
    total_ref, spread = rest[-2:]
    place(pair_ref, code_ref, blocks, first, spread)
    rows = 512
    for start in range(0, turn_ref.shape[0], rows):
        here = slice(start, start + rows)
        new = jnp.dot(turn_ref[here, :], spread[...], preferred_element_type=jnp.float32)
        total_ref[here, :] = rest[0][here, :] + new if more else new

def last_kernel(pair_ref, code_ref, turn_ref, *refs, first, n_blocks, scale):
    blocks, (held_ref, out_ref, spread, ready, sems) = refs[:n_blocks], refs[n_blocks:]
    place(pair_ref, code_ref, blocks, first, spread)
    copies = sems.shape[0]
    columns = ready.shape[0] // copies
    rows = 2 * columns
    sent = []
    for number in range(copies):
        here = slice(number * rows, (number + 1) * rows)
        new = jnp.dot(turn_ref[here, :], spread[...], preferred_element_type=jnp.float32)
        total = ((held_ref[here, :] + new) * scale).astype(jnp.bfloat16)
        there = pl.ds(number * columns, columns)
        ready[there] = total.reshape((columns,) + ready.shape[1:])
        copy = pltpu.make_async_copy(ready.at[there], out_ref.at[there], sems.at[number])
        copy.start()
        sent.append(copy)
    for copy in sent:
        copy.wait()

def part(pairs, code, turn, blocks, held, first, scale=None, mark=None):
    tiles = code.shape[0]
    rows, depth = turn.shape
    n = tiles * LANES
    operands = (pairs, code, turn, *blocks, mark if held is None else held)
    specs = [SMEM] + [VMEM] * (len(operands) - 1)
    scratch = [pltpu.VMEM((depth, n), jnp.bfloat16)]
    params = pltpu.CompilerParams(vmem_limit_bytes=(6 if scale is None else 10) << 20)
    if scale is None:
        return pl.pallas_call(
            functools.partial(
                part_kernel, first=first, n_blocks=len(blocks), more=held is not None
            ),
            out_shape=jax.ShapeDtypeStruct((rows, n), jnp.float32),
            in_specs=specs,
            out_specs=VMEM,
            scratch_shapes=scratch,
            input_output_aliases={} if held is None else {len(operands) - 1: 0},
            compiler_params=params,
            name="part",
        )(*operands)
    shape = jax.ShapeDtypeStruct((rows // 2, 2, n), jnp.bfloat16)
    return pl.pallas_call(
        functools.partial(last_kernel, first=first, n_blocks=len(blocks), scale=scale),
        out_shape=shape,
        in_specs=specs,
        out_specs=pl.BlockSpec(memory_space=pl.ANY),
        scratch_shapes=scratch
        + [pltpu.VMEM(shape.shape, shape.dtype), pltpu.SemaphoreType.DMA((8,))],
        compiler_params=params,
        name="last",
    )(*operands)

def pick(table, index):
    hot = index[:, None] == jnp.arange(table.shape[0], dtype=jnp.int32)[None, :]
    return jnp.sum(jnp.where(hot[:, :, None], table[None], 0), axis=1)

def twiddles(rates, first_column, columns):
    step_angle = 2.0 * math.pi / COLS
    coarse_k = first_column + FINE_K * jnp.arange(columns // FINE_K, dtype=jnp.int32)
    coarse = ((rates[None, :] * coarse_k[:, None]) % COLS).astype(jnp.float32) * step_angle
    row = jnp.arange(2 * FINE_K, dtype=jnp.int32)
    turn = rates[None, :] * (row // 2)[:, None] + (COLS - (COLS // 4) * (row % 2))[:, None]
    within = (turn % COLS).astype(jnp.float32) * step_angle
    return (
        jnp.stack([jnp.cos(coarse), jnp.sin(coarse)])[:, :, None, :],
        jnp.stack([jnp.cos(within), jnp.sin(within)]),
    )

def body(echoes, pulse_ids, bin_start, live_count, wavenum, interp):
    blocks = lax.axis_size(ANG)
    ang_index = lax.axis_index(ANG)
    n_rows = lax.axis_size(ROW)
    ring = lax.axis_size("z")
    tiles_mine = interp.shape[0]
    block_pulses = echoes.shape[0]
    foot_len = pulse_ids.shape[1]
    per_block = foot_len // blocks
    col_dev = COLS // blocks
    first_entry = ang_index * per_block

    my_ids = lax.dynamic_slice_in_dim(pulse_ids, first_entry, per_block, 1)
    my_starts = lax.dynamic_slice_in_dim(bin_start, first_entry, per_block, 1)
    my_live = lax.dynamic_slice_in_dim(live_count, ang_index, 1, 1)
    packed = pack(echoes, my_ids - ang_index * block_pulses, my_starts, my_live)
    got = lax.all_to_all(packed.reshape(n_rows, -1, LANES), ROW, 0, 0, tiled=True)
    my_tiles = lax.axis_index(ROW) * tiles_mine
    back = (-lax.dynamic_slice(bin_start, (my_tiles, first_entry), (tiles_mine, per_block))) & (LANES - 1)
    mine = focus(back, got, interp.swapaxes(1, 2))

    yh, z, core = (lax.axis_index(name) for name in ANG)
    half = ring // 2
    shift, side = [0, 0, -1, 1], [0, 1, 0, 0]
    for step in range(2, half):
        shift += [1 - step, step - 1, -step, step]
        side += [1, 1, 0, 0]
    shift = jnp.array(shift + [1 - half, half - 1, half, half], jnp.int32)
    side = jnp.array(side + [1, 1, 0, 1], jnp.int32)
    pairs = ((z + shift) % ring) * 2 + (core ^ side)
    order = (pairs[:, None] + 2 * ring * (yh ^ jnp.arange(2, dtype=jnp.int32))[None, :]).reshape(-1)
    tile_ids = lax.dynamic_slice_in_dim(
        pulse_ids, my_tiles, tiles_mine, 0
    ).reshape(tiles_mine, 2, 2 * ring, per_block)
    tile_ids = jnp.where(yh == 0, tile_ids, tile_ids[:, ::-1]) % block_pulses
    tile_ids = tile_ids + block_pulses * jnp.arange(2, dtype=jnp.int32)[None, :, None, None]
    code = tile_ids.transpose(0, 2, 1, 3)[..., None] + 2 * block_pulses * jnp.arange(2, dtype=jnp.int32)
    code = code.reshape(tiles_mine, 2 * ring, 1, 4 * per_block)
    rates = pick(wavenum.reshape(blocks, block_pulses), order).reshape(-1)
    coarse, fine = twiddles(rates, ang_index * col_dev, col_dev)

    mark, *tables = turns(coarse, fine, half)

    swap = [(0, 1), (1, 0)]
    ahead = [(i, (i + 1) % ring) for i in range(ring)]
    behind = [(i, (i - 1) % ring) for i in range(ring)]
    other = lax.ppermute(mine, "yh", swap)
    other, mark = lax.optimization_barrier((other, mark))

    forward = backward = jnp.concatenate([mine, other], 0)
    near = [forward]
    far, total = [], None
    for step in range(1, half):
        arriving = lax.ppermute(forward, "z", ahead), lax.ppermute(backward, "z", behind)
        if step > 1:
            total = part(
                pairs, code, tables[step - 2], blocks, total, 4 * (step - 2), mark=mark
            )
            *leaving, total = lax.optimization_barrier((*near, total))
            far = [lax.ppermute(block, "core", swap) for block in leaving]
            forward, backward, total = lax.optimization_barrier((*arriving, total))
        else:
            far = [lax.ppermute(block, "core", swap) for block in near]
            forward, backward = lax.optimization_barrier(arriving)
        blocks = ([*near] if step == 1 else []) + far + [forward, backward]
        near = [forward, backward]
    opposite = lax.ppermute(forward, "z", ahead)
    crossing = [
        (2 * i + side, 2 * ((i - 1) % ring) + 1 - side) for i in range(ring) for side in (0, 1)
    ]
    across = lax.ppermute(backward, ("z", "core"), crossing)
    far = [lax.ppermute(block, "core", swap) for block in near]
    total = part(pairs, code, tables[half - 2], blocks, total, 4 * (half - 2))
    opposite, across, total = lax.optimization_barrier((opposite, across, total))
    blocks = far + [opposite, across]
    return part(pairs, code, tables[half - 1], blocks, total, 4 * (half - 1), foot_len ** (-0.5))


def solution(mesh):
    finer = Mesh(mesh.devices.reshape(2, -1, 2, 4, 2), FINE)
    return jax.shard_map(
        body,
        mesh=finer,
        in_specs=(P(ANG, None, ROW), P(), P(), P(), P(), P(ROW, None, None)),
        out_specs=P(ANG, None, ROW),
        check_vma=False,
    )
```

```python
import functools
import math

import jax
import jax.numpy as jnp
from jax import lax
from jax.experimental import pallas as pl
from jax.experimental.pallas import tpu as pltpu
from jax.sharding import Mesh
from jax.sharding import PartitionSpec as P

COLS = 32768
LANES = 128
FINE_K = 32
ANG = ("yh", "z", "core")
ROW = ("x", "yl")
FINE = ("yh", "z", "core", "x", "yl")
SMEM = pl.BlockSpec(memory_space=pltpu.SMEM)
VMEM = pl.BlockSpec(memory_space=pltpu.VMEM)

def pack_kernel(word_ref, bins_ref, out_ref):
    tiles, per_block = word_ref.shape
    _, parts, lanes = bins_ref.shape
    lane = lax.broadcasted_iota(jnp.int32, (parts, lanes), 1)
    at_once = 8

    def take(step, _):
        for u in range(at_once):
            for entry in range(per_block):
                word = word_ref[step * at_once + u, entry]
                row = word >> 7
                low = bins_ref[row].astype(jnp.float32)
                high = bins_ref[row + 1].astype(jnp.float32)
                cut = jnp.where(lane >= (word & (lanes - 1)), low, high)
                out_ref[(step * at_once + u) * per_block + entry] = cut.astype(out_ref.dtype)
        return 0

    lax.fori_loop(0, tiles // at_once, take, 0)


def pack(echoes, ids, starts, live):
    pulses, parts, bins = echoes.shape
    panels = bins // LANES
    tiles, per_block = ids.shape
    rows = echoes.reshape(pulses, parts, panels, LANES).transpose(0, 2, 1, 3)
    rows = jnp.pad(rows, ((0, 0), (1, 1), (0, 0), (0, 0)))
    offs = starts - lax.axis_index(ROW) * bins
    used = jnp.arange(per_block, dtype=jnp.int32)[None, :] < live
    inside = used & (offs > -LANES) & (offs < bins)
    first = jnp.where(inside, ids * (panels + 2) + (offs >> 7) + 1, panels + 1)
    word = first * LANES + (offs & (LANES - 1))
    return pl.pallas_call(
        pack_kernel,
        out_shape=jax.ShapeDtypeStruct((tiles * per_block, parts, LANES), echoes.dtype),
        in_specs=[SMEM, VMEM],
        out_specs=VMEM,
        compiler_params=pltpu.CompilerParams(vmem_limit_bytes=4 << 20),
        name="pack",
    )(word, rows.reshape(pulses * (panels + 2), parts, LANES))


def focus_kernel(back_ref, got_ref, turned_ref, out_ref, panels):
    tiles, per_block = back_ref.shape
    rows = out_ref.shape[0] // tiles
    total = got_ref[0]
    for source in range(1, got_ref.shape[0]):
        total += got_ref[source]
    panels[...] = total.astype(jnp.float32)
    for tile in range(tiles):
        windows = []
        for entry in range(per_block):
            at = tile * rows + entry * 2
            windows.append(pltpu.roll(panels[at : at + 2, :], back_ref[tile, entry], 1))
        out_ref[tile * rows : (tile + 1) * rows, :] = jnp.dot(
            jnp.concatenate(windows, 0).astype(jnp.bfloat16),
            turned_ref[tile],
            preferred_element_type=jnp.float32,
        ).astype(jnp.bfloat16)


def focus(back, got, turned):
    return pl.pallas_call(
        focus_kernel,
        out_shape=jax.ShapeDtypeStruct(got.shape[1:], jnp.bfloat16),
        in_specs=[SMEM, VMEM, VMEM],
        out_specs=VMEM,
        scratch_shapes=[pltpu.VMEM(got.shape[1:], jnp.float32)],
        compiler_params=pltpu.CompilerParams(vmem_limit_bytes=4 << 20),
        name="focus",
    )(back, got, turned)


def place(pair_ref, code_ref, blocks, first, spread):
    tiles = code_ref.shape[0]
    half = spread.shape[0] // 2
    slots = 2 * 32
    wide = code_ref.shape[3]
    side = wide // 2
    row = lax.broadcasted_iota(jnp.int32, (2 * slots, wide), 0)
    for number, ref in enumerate(blocks):
        pair = pair_ref[first + number]
        for tile in range(tiles):
            entries = [ref[(s * tiles + tile) * side : (s * tiles + tile + 1) * side, :] for s in (0, 1)]
            hot = jnp.where(row == code_ref[tile, pair], 1.0, 0.0).astype(jnp.bfloat16)
            placed = jnp.dot(
                hot, jnp.concatenate(entries, 0), preferred_element_type=jnp.float32
            ).astype(jnp.bfloat16)
            columns = slice(tile * LANES, (tile + 1) * LANES)
            spread[number * slots : (number + 1) * slots, columns] = placed[:slots]
            spread[half + number * slots : half + (number + 1) * slots, columns] = placed[slots:]

def turn_kernel(coarse_ref, fine_ref, mark_ref, *out_refs):
    pulses = coarse_ref.shape[3] // len(out_refs)
    rows = fine_ref.shape[1]

    def step(number, _):
        here = pl.ds(pl.multiple_of(number * rows, rows), rows)
        for which, out_ref in enumerate(out_refs):
            columns = pl.ds(which * pulses, pulses)
            coarse_c, coarse_s = coarse_ref[0, number, :, columns], coarse_ref[1, number, :, columns]
            fine_c, fine_s = fine_ref[0, :, columns], fine_ref[1, :, columns]
            out_ref[here, :pulses] = (coarse_c * fine_c - coarse_s * fine_s).astype(jnp.bfloat16)
            out_ref[here, pulses:] = (-coarse_s * fine_c - coarse_c * fine_s).astype(jnp.bfloat16)
        return 0

    lax.fori_loop(0, coarse_ref.shape[1], step, 0, unroll=4)
    mark_ref[...] = jnp.zeros(mark_ref.shape, mark_ref.dtype)

def turns(coarse, fine, parts):
    rows = coarse.shape[1] * fine.shape[1]
    shape = jax.ShapeDtypeStruct((rows, 2 * coarse.shape[3] // parts), jnp.bfloat16)
    return pl.pallas_call(
        turn_kernel,
        out_shape=[jax.ShapeDtypeStruct((8, LANES), jnp.float32)] + [shape] * parts,
        in_specs=[VMEM] * 2,
        out_specs=[VMEM] * (parts + 1),
        compiler_params=pltpu.CompilerParams(vmem_limit_bytes=2 << 20),
        name="turns",
    )(coarse, fine)

def part_kernel(pair_ref, code_ref, turn_ref, *refs, first, n_blocks, more):
    blocks, rest = refs[:n_blocks], refs[n_blocks:]
    total_ref, spread = rest[-2:]
    place(pair_ref, code_ref, blocks, first, spread)
    rows = 1024
    for start in range(0, turn_ref.shape[0], rows):
        here = slice(start, start + rows)
        new = jnp.dot(turn_ref[here, :], spread[...], preferred_element_type=jnp.float32)
        total_ref[here, :] = rest[0][here, :] + new if more else new

def last_kernel(pair_ref, code_ref, turn_ref, *refs, first, n_blocks, scale):
    blocks, (held_ref, out_ref, spread, ready, sems) = refs[:n_blocks], refs[n_blocks:]
    place(pair_ref, code_ref, blocks, first, spread)
    copies = sems.shape[0]
    columns = ready.shape[0] // copies
    rows = 2 * columns
    sent = []
    for number in range(copies):
        here = slice(number * rows, (number + 1) * rows)
        new = jnp.dot(turn_ref[here, :], spread[...], preferred_element_type=jnp.float32)
        total = ((held_ref[here, :] + new) * scale).astype(jnp.bfloat16)
        there = pl.ds(number * columns, columns)
        ready[there] = total.reshape((columns,) + ready.shape[1:])
        copy = pltpu.make_async_copy(ready.at[there], out_ref.at[there], sems.at[number])
        copy.start()
        sent.append(copy)
    for copy in sent:
        copy.wait()

def part(pairs, code, turn, blocks, held, first, scale=None, mark=None):
    tiles = code.shape[0]
    rows, depth = turn.shape
    n = tiles * LANES
    operands = (pairs, code, turn, *blocks, mark if held is None else held)
    specs = [SMEM] + [VMEM] * (len(operands) - 1)
    scratch = [pltpu.VMEM((depth, n), jnp.bfloat16)]
    params = pltpu.CompilerParams(vmem_limit_bytes=(6 if scale is None else 10) << 20)
    if scale is None:
        return pl.pallas_call(
            functools.partial(
                part_kernel, first=first, n_blocks=len(blocks), more=held is not None
            ),
            out_shape=jax.ShapeDtypeStruct((rows, n), jnp.float32),
            in_specs=specs,
            out_specs=VMEM,
            scratch_shapes=scratch,
            input_output_aliases={} if held is None else {len(operands) - 1: 0},
            compiler_params=params,
            name="part",
        )(*operands)
    shape = jax.ShapeDtypeStruct((rows // 2, 2, n), jnp.bfloat16)
    return pl.pallas_call(
        functools.partial(last_kernel, first=first, n_blocks=len(blocks), scale=scale),
        out_shape=shape,
        in_specs=specs,
        out_specs=pl.BlockSpec(memory_space=pl.ANY),
        scratch_shapes=scratch
        + [pltpu.VMEM(shape.shape, shape.dtype), pltpu.SemaphoreType.DMA((8,))],
        compiler_params=params,
        name="last",
    )(*operands)

def pick(table, index):
    hot = index[:, None] == jnp.arange(table.shape[0], dtype=jnp.int32)[None, :]
    return jnp.sum(jnp.where(hot[:, :, None], table[None], 0), axis=1)

def twiddles(rates, first_column, columns):
    step_angle = 2.0 * math.pi / COLS
    coarse_k = first_column + FINE_K * jnp.arange(columns // FINE_K, dtype=jnp.int32)
    coarse = ((rates[None, :] * coarse_k[:, None]) % COLS).astype(jnp.float32) * step_angle
    row = jnp.arange(2 * FINE_K, dtype=jnp.int32)
    turn = rates[None, :] * (row // 2)[:, None] + (COLS - (COLS // 4) * (row % 2))[:, None]
    within = (turn % COLS).astype(jnp.float32) * step_angle
    return (
        jnp.stack([jnp.cos(coarse), jnp.sin(coarse)])[:, :, None, :],
        jnp.stack([jnp.cos(within), jnp.sin(within)]),
    )

def body(echoes, pulse_ids, bin_start, live_count, wavenum, interp):
    blocks = lax.axis_size(ANG)
    ang_index = lax.axis_index(ANG)
    n_rows = lax.axis_size(ROW)
    ring = lax.axis_size("z")
    tiles_mine = interp.shape[0]
    block_pulses = echoes.shape[0]
    foot_len = pulse_ids.shape[1]
    per_block = foot_len // blocks
    col_dev = COLS // blocks
    first_entry = ang_index * per_block

    my_ids = lax.dynamic_slice_in_dim(pulse_ids, first_entry, per_block, 1)
    my_starts = lax.dynamic_slice_in_dim(bin_start, first_entry, per_block, 1)
    my_live = lax.dynamic_slice_in_dim(live_count, ang_index, 1, 1)
    packed = pack(echoes, my_ids - ang_index * block_pulses, my_starts, my_live)
    got = lax.all_to_all(packed.reshape(n_rows, -1, LANES), ROW, 0, 0, tiled=True)
    my_tiles = lax.axis_index(ROW) * tiles_mine
    back = (-lax.dynamic_slice(bin_start, (my_tiles, first_entry), (tiles_mine, per_block))) & (LANES - 1)
    mine = focus(back, got, interp.swapaxes(1, 2))

    yh, z, core = (lax.axis_index(name) for name in ANG)
    half = ring // 2
    shift, side = [0, 0, -1, 1], [0, 1, 0, 0]
    for step in range(2, half):
        shift += [1 - step, step - 1, -step, step]
        side += [1, 1, 0, 0]
    shift = jnp.array(shift + [1 - half, half - 1, half, half], jnp.int32)
    side = jnp.array(side + [1, 1, 0, 1], jnp.int32)
    pairs = ((z + shift) % ring) * 2 + (core ^ side)
    order = (pairs[:, None] + 2 * ring * (yh ^ jnp.arange(2, dtype=jnp.int32))[None, :]).reshape(-1)
    tile_ids = lax.dynamic_slice_in_dim(
        pulse_ids, my_tiles, tiles_mine, 0
    ).reshape(tiles_mine, 2, 2 * ring, per_block)
    tile_ids = jnp.where(yh == 0, tile_ids, tile_ids[:, ::-1]) % block_pulses
    tile_ids = tile_ids + block_pulses * jnp.arange(2, dtype=jnp.int32)[None, :, None, None]
    code = tile_ids.transpose(0, 2, 1, 3)[..., None] + 2 * block_pulses * jnp.arange(2, dtype=jnp.int32)
    code = code.reshape(tiles_mine, 2 * ring, 1, 4 * per_block)
    rates = pick(wavenum.reshape(blocks, block_pulses), order).reshape(-1)
    coarse, fine = twiddles(rates, ang_index * col_dev, col_dev)

    mark, *tables = turns(coarse, fine, half)

    swap = [(0, 1), (1, 0)]
    ahead = [(i, (i + 1) % ring) for i in range(ring)]
    behind = [(i, (i - 1) % ring) for i in range(ring)]
    other = lax.ppermute(mine, "yh", swap)
    other, mark = lax.optimization_barrier((other, mark))

    forward = backward = jnp.concatenate([mine, other], 0)
    near = [forward]
    far, total = [], None
    for step in range(1, half):
        arriving = lax.ppermute(forward, "z", ahead), lax.ppermute(backward, "z", behind)
        if step > 1:
            total = part(
                pairs, code, tables[step - 2], blocks, total, 4 * (step - 2), mark=mark
            )
            *leaving, total = lax.optimization_barrier((*near, total))
            far = [lax.ppermute(block, "core", swap) for block in leaving]
            forward, backward, total = lax.optimization_barrier((*arriving, total))
        else:
            far = [lax.ppermute(block, "core", swap) for block in near]
            forward, backward = lax.optimization_barrier(arriving)
        blocks = ([*near] if step == 1 else []) + far + [forward, backward]
        near = [forward, backward]
    opposite = lax.ppermute(forward, "z", ahead)
    crossing = [
        (2 * i + side, 2 * ((i - 1) % ring) + 1 - side) for i in range(ring) for side in (0, 1)
    ]
    across = lax.ppermute(backward, ("z", "core"), crossing)
    far = [lax.ppermute(block, "core", swap) for block in near]
    total = part(pairs, code, tables[half - 2], blocks, total, 4 * (half - 2))
    opposite, across, total = lax.optimization_barrier((opposite, across, total))
    blocks = far + [opposite, across]
    return part(pairs, code, tables[half - 1], blocks, total, 4 * (half - 1), foot_len ** (-0.5))


def solution(mesh):
    finer = Mesh(mesh.devices.reshape(2, -1, 2, 4, 2), FINE)
    return jax.shard_map(
        body,
        mesh=finer,
        in_specs=(P(ANG, None, ROW), P(), P(), P(), P(), P(ROW, None, None)),
        out_specs=P(ANG, None, ROW),
        check_vma=False,
    )
```
